512 devices in a mesh: cell: 128 (over z, x, core), lag: 4 (over y).
Axes of the slice: x: 4, y: 4, z: 16, core: 2. Of those that a mesh axis runs over, the one named last changes fastest.
Arguments:
- green: bfloat16 [32, 640, 32768], P('lag', None, 'cell'), may hold values from -0.0078125 to 0.0078125
- source: bfloat16 [8, 48, 32768], P(None, None, 'cell'), may hold values from -6 to 6
- observed: float32 [8, 48, 640], replicated, may hold values from -6 to 6
- lag_gaps: int32 [31], replicated, may hold values from 1 to 2, 47 in all
- huber_level: int32 [640], replicated, may hold values from 0 to 7
Outputs:
- gradient: float32 [8, 48, 32768], P(None, 'lag', 'cell')
The draws below stay inside these ranges and needn't reach their ends.
Inputs may be any that keep to these rules, and one draw needn't show every extreme that they name: `lag_gaps`: the gaps sum to 47.
All inputs are finite; a program needn't handle non-finite values.
Results may differ from the reference program's by a relative error of at most 0.0034.
Values may be sent and summed in bfloat16 or wider, within the bound.
No kernel may reach another device: no remote copies, remote signals or barrier semaphores. Data moves between devices by JAX's collectives and lax.ppermute only.
A program may use at most 64 MiB of HBM per device.

```python
import math
import jax
import jax.numpy as jnp
import numpy as np
from jax import lax

SENS = 640
NT = 48
RHS = 8
CELLS = 32768
LAGS = 32
GAP_MOST = 2


def plant(drawn, own_key, low, high):
    extent = drawn.shape
    index_at = [jax.random.randint(jax.random.fold_in(own_key, axis), (), 0, extent[axis]) for axis in range(len(extent))]
    drawn = drawn.at[tuple(index_at)].set(low)
    longest = extent.index(max(extent))
    index_at[longest] = (index_at[longest] + 1) % extent[longest]
    return drawn.at[tuple(index_at)].set(high)


def shard_levels(stream_key, extent, split, low, high):
    loudness, own = 1.0, jax.random.fold_in(stream_key, 6)
    for position, shards_of in split:
        draws = jnp.exp(jax.random.uniform(jax.random.fold_in(own, position), (shards_of,), jnp.float32, low / len(split), high / len(split)))
        loudness = loudness * jnp.repeat(draws, extent[position] // shards_of).reshape([-1 if axis == position else 1 for axis in range(len(extent))])
    return loudness


def profile(number_of, total, bound, slope):
    weights = [(1 << 20) // math.isqrt(standing ** slope) + 1 for standing in range(2, number_of + 1)]
    surplus, holding = total - bound - (number_of - 1), [1] * (number_of - 1)
    while surplus > 0:
        candidates = [i for i in range(number_of - 1) if holding[i] < bound]
        mass, budget = sum([weights[i] for i in candidates]), surplus
        for i in candidates:
            more = min(bound - holding[i], max(1, budget * weights[i] // mass), surplus)
            holding[i] = holding[i] + more
            surplus = surplus - more
    return np.array([bound] + holding)


def ragged(rng, amount, total, most, skew):
    if amount == 2:
        one = jax.random.randint(rng, (), max(1, total - most), min(most, total - 1) + 1)
        return jnp.stack([one, total - one])
    sizes = jnp.asarray(profile(amount, total, most, skew), jnp.int32)
    couples = (amount - 1) // 2
    source_of, sink = sizes[1:1 + 2 * couples:2], sizes[2:2 + 2 * couples:2]
    room = jnp.minimum(source_of - 1, most - sink)
    moved = jax.random.randint(jax.random.fold_in(rng, 1), (couples,), 0, 1 << 20) % (room + 1)
    sizes = sizes.at[1:1 + 2 * couples:2].set(source_of - moved).at[2:2 + 2 * couples:2].set(sink + moved)
    return sizes[jax.random.permutation(jax.random.fold_in(rng, 2), amount)]


def gaussian(stream_key, shape, scale, bound, cuts=(), held_as=jnp.bfloat16):
    factor_of = shard_levels(stream_key, shape, cuts, -0.22, 0.18) if cuts else 1.0
    array = jax.random.normal(stream_key, shape, jnp.float32) * scale * factor_of
    return jnp.minimum(jnp.maximum(array, -bound), bound).astype(held_as)


def setup_inputs(seed: int = 0) -> dict:
    key_list = jax.random.split(jax.random.key(seed), 6)
    return {
        "green": gaussian(key_list[0], (LAGS, SENS, CELLS), (CELLS * LAGS // 2) ** -0.5, 0.0078125, ((0, 4), (2, 128))),
        "source": gaussian(key_list[1], (RHS, NT, CELLS), 1.0, 6.0, ((2, 128),)),
        "observed": gaussian(key_list[2], (RHS, NT, SENS), 1.0, 6.0, (), jnp.float32),
        "lag_gaps": ragged(key_list[3], LAGS - 1, NT - 1, GAP_MOST, 0).astype(jnp.int32),
        "huber_level": plant(jax.random.randint(key_list[4], (SENS,), 0, 8), jax.random.fold_in(key_list[4], 1), 0, 7).astype(jnp.int32),
    }


def reference(green, source, observed, lag_gaps, huber_level):
    lag_of = jnp.concatenate([jnp.zeros((1,), jnp.int32), jnp.cumsum(lag_gaps).astype(jnp.int32)])
    zeros_src = jnp.zeros((RHS, NT, CELLS), jnp.bfloat16)
    padded = jnp.concatenate([zeros_src, source], axis=1)

    def fwd_step(total, item):
        block, lag = item
        shifted = lax.dynamic_slice_in_dim(padded, (NT - lag).astype(jnp.int32), NT, 1)
        return total + jnp.einsum("rtc,sc->rts", shifted, block, preferred_element_type=jnp.float32), None

    predicted, _ = lax.scan(fwd_step, jnp.zeros((RHS, NT, SENS), jnp.float32), (green, lag_of))
    threshold = 0.3 * (huber_level.astype(jnp.float32) + 1.0)
    misfit = predicted - observed
    weighted = (misfit * threshold / jnp.maximum(jnp.abs(misfit), threshold)).astype(jnp.bfloat16)
    later = jnp.concatenate([weighted, jnp.zeros((RHS, NT, SENS), jnp.bfloat16)], axis=1)

    def adj_step(total, item):
        block, lag = item
        window = lax.dynamic_slice_in_dim(later, lag.astype(jnp.int32), NT, 1)
        return total + jnp.einsum("rts,sc->rtc", window, block, preferred_element_type=jnp.float32), None

    gradient, _ = lax.scan(adj_step, jnp.zeros((RHS, NT, CELLS), jnp.float32), (green, lag_of))
    return gradient
```

```python
import jax
import jax.numpy as jnp
from jax import lax
from jax.experimental import pallas as pl
from jax.experimental.pallas import tpu as pltpu
from jax.sharding import Mesh, PartitionSpec as P

PLANE = ("x", "c", "y")
WIRE = jnp.float32
INTERPRET = False


def first_lag(place_ref, gaps_ref, own_count):
    before = place_ref[0] * own_count

    def add(i, total):
        return total + jnp.where(i < before, gaps_ref[i], 0)

    return lax.fori_loop(0, gaps_ref.shape[0], add, jnp.int32(0))


def next_lag(place_ref, gaps_ref, lag, block, own_count):
    at = jnp.minimum(place_ref[0] * own_count + block, gaps_ref.shape[0] - 1)
    return lag + gaps_ref[at]


def forward_kernel(place_ref, gaps_ref, source_ref, green_ref, out_ref, early, total, stage, lag_ref):
    block, blocks = pl.program_id(0), pl.num_programs(0)
    rows, steps, _ = source_ref.shape
    height = rows * steps

    @pl.when(block == 0)
    def _():
        lag_ref[0] = first_lag(place_ref, gaps_ref, blocks)
        total[...] = jnp.zeros_like(total)
        for i in range(early.shape[0]):
            lane = early.shape[2]
            early[i, pl.ds(0, height), :] = jnp.zeros((height, lane), early.dtype)
            for r in range(rows):
                piece = source_ref[r, :, i * lane:(i + 1) * lane].astype(jnp.float32)
                early[i, pl.ds(height + r, steps, stride=rows), :] = piece

    lag = lag_ref[0]
    start = pl.multiple_of((steps - lag) * rows, rows)
    shifted = [early[i, pl.ds(start, height), :].astype(jnp.bfloat16) for i in range(early.shape[0])]
    shifted = jnp.concatenate(shifted, axis=1)
    total[...] += lax.dot_general(
        shifted, green_ref[0], (((1,), (1,)), ((), ())), preferred_element_type=jnp.float32
    )
    lag_ref[0] = next_lag(place_ref, gaps_ref, lag, block, blocks)

    @pl.when(block == blocks - 1)
    def _():
        owners, kept, lanes = out_ref.shape
        part = height // owners
        stage[...] = jnp.zeros_like(stage)
        for q in range(owners):
            for j in range(total.shape[1] // lanes):
                stage[pl.ds(j * part, part), :] = total[pl.ds(q * part, part), pl.ds(j * lanes, lanes)]
            out_ref[q] = stage[...].astype(out_ref.dtype)


def forward(place, gaps, source, green, owners, kept):
    rows, steps, cells = source.shape
    blocks, sensors, _ = green.shape
    height = rows * steps
    return pl.pallas_call(
        forward_kernel,
        grid_spec=pltpu.PrefetchScalarGridSpec(
            num_scalar_prefetch=2,
            grid=(blocks,),
            in_specs=[
                pl.BlockSpec((rows, steps, cells), lambda k, *_: (0, 0, 0)),
                pl.BlockSpec((1, sensors, cells), lambda k, *_: (k, 0, 0)),
            ],
            out_specs=pl.BlockSpec((owners, kept, 128), lambda k, *_: (0, 0, 0)),
            scratch_shapes=[
                pltpu.VMEM((pl.cdiv(cells, 128), 2 * height, min(cells, 128)), jnp.float32),
                pltpu.VMEM((height, sensors), jnp.float32),
                pltpu.VMEM((kept, 128), jnp.float32),
                pltpu.SMEM((1,), jnp.int32),
            ],
        ),
        out_shape=jax.ShapeDtypeStruct((owners, kept, 128), WIRE),
        interpret=INTERPRET,
        name="forward",
    )(place, gaps, source, green)


def adjoint_kernel(place_ref, gaps_ref, weighted_ref, green_ref, out_ref, late, lag_ref):
    block, blocks = pl.program_id(0), pl.num_programs(0)
    owners, _, lanes = weighted_ref.shape
    height = out_ref.shape[0]
    part = height // owners

    @pl.when(block == 0)
    def _():
        lag_ref[0] = first_lag(place_ref, gaps_ref, blocks)
        out_ref[...] = jnp.zeros_like(out_ref)
        late[pl.ds(height, height), :] = jnp.zeros((height, late.shape[1]), late.dtype)
        for q in range(owners):
            piece = weighted_ref[q].astype(jnp.float32)
            for j in range(late.shape[1] // lanes):
                late[pl.ds(q * part, part), pl.ds(j * lanes, lanes)] = piece[j * part:(j + 1) * part]

    lag = lag_ref[0]
    rows = height // 48
    start = pl.multiple_of(lag * rows, rows)
    window = late[pl.ds(start, height), :].astype(jnp.bfloat16)
    out_ref[...] += jnp.dot(window, green_ref[0], preferred_element_type=jnp.float32)
    lag_ref[0] = next_lag(place_ref, gaps_ref, lag, block, blocks)


def adjoint(place, gaps, weighted, green, height):
    blocks, sensors, cells = green.shape
    owners, kept, lanes = weighted.shape
    return pl.pallas_call(
        adjoint_kernel,
        grid_spec=pltpu.PrefetchScalarGridSpec(
            num_scalar_prefetch=2,
            grid=(blocks,),
            in_specs=[
                pl.BlockSpec((owners, kept, lanes), lambda k, *_: (0, 0, 0)),
                pl.BlockSpec((1, sensors, cells), lambda k, *_: (k, 0, 0)),
            ],
            out_specs=pl.BlockSpec((height, cells), lambda k, *_: (0, 0)),
            scratch_shapes=[
                pltpu.VMEM((2 * height, sensors), jnp.float32),
                pltpu.SMEM((1,), jnp.int32),
            ],
        ),
        out_shape=jax.ShapeDtypeStruct((height, cells), jnp.float32),
        interpret=INTERPRET,
        name="adjoint",
    )(place, gaps, weighted, green)


def body(green, source, observed, lag_gaps, huber_level):
    rows, steps, cells = source.shape
    sensors = green.shape[1]
    depth, owners, groups = lax.axis_size("z"), lax.axis_size(PLANE), lax.axis_size("y")
    kept = depth * 4
    part = rows * steps // owners
    place = lax.axis_index("y")[None]

    sent = forward(place, lag_gaps, source, green, owners, kept)
    sent = lax.all_to_all(sent, PLANE, 0, 0, tiled=True)
    plane_sum = jnp.sum(sent.astype(jnp.float32), axis=0).reshape(depth, 4, 128)
    summed = jnp.sum(lax.all_to_all(plane_sum, "z", 0, 0, tiled=True), axis=0)

    p = jnp.minimum(lax.axis_index("z"), depth - 2)
    j, h = p // 3, p % 3
    row = lax.axis_index(PLANE) * part + 4 * h
    seen = lax.dynamic_slice(observed, (row % rows, row // rows, 128 * j), (4, 1, 128)).reshape(4, 128)
    level = lax.dynamic_slice(huber_level, (128 * j,), (128,))
    threshold = 0.3 * (level.astype(jnp.float32) + 1.0)[None]
    misfit = summed - seen
    own = (misfit * threshold / jnp.maximum(jnp.abs(misfit), threshold)).astype(jnp.bfloat16)

    own = lax.all_to_all(jnp.broadcast_to(own[None], (depth, 4, 128)), "z", 0, 0, tiled=True)
    own = jnp.broadcast_to(own.reshape(1, kept, 128), (owners, kept, 128))
    weighted = lax.all_to_all(own, PLANE, 0, 0, tiled=True)

    terms = adjoint(place, lag_gaps, weighted, green, rows * steps)
    terms = terms.reshape(groups, steps // groups, rows, cells)
    terms = jnp.sum(lax.all_to_all(terms, "y", 0, 0, tiled=True), axis=0)
    return terms.transpose(1, 0, 2)


def solution(mesh):
    fine = Mesh(mesh.devices.reshape(16, 4, 2, 4), ("z", "x", "c", "y"))
    cell = ("z", "x", "c")
    in_specs = (P("y", None, cell), P(None, None, cell), P(), P(), P())
    out_specs = P(None, "y", cell)
    return jax.shard_map(body, mesh=fine, in_specs=in_specs, out_specs=out_specs, check_vma=False)
```

```python
import functools

import jax
import jax.numpy as jnp
from jax import lax
from jax.experimental import pallas as pl
from jax.experimental.pallas import tpu as pltpu
from jax.sharding import Mesh, PartitionSpec as P

PLANE = ("x", "c", "y")
TALL, WIDE = 64, 128
WIRE = jnp.bfloat16
VMEM = pl.BlockSpec(memory_space=pltpu.VMEM)
SMEM = pl.BlockSpec(memory_space=pltpu.SMEM)
LIMIT = pltpu.CompilerParams(vmem_limit_bytes=20 << 20)


def lags(place_ref, gaps_ref, own_count):
    before = place_ref[0] * own_count
    lag = jnp.int32(0)
    for i in range(gaps_ref.shape[0] - own_count + 1):
        lag = lag + jnp.where(i < before, gaps_ref[i], 0)
    found = [lag]
    for i in range(own_count - 1):
        lag = lag + gaps_ref[before + i]
        found.append(lag)
    return found


def cut(value, out_ref):
    up = value.shape[0] // TALL
    for q in range(out_ref.shape[0]):
        j, a = q // up, q % up
        if j < value.shape[1] // WIDE:
            block = value[a * TALL:(a + 1) * TALL, j * WIDE:(j + 1) * WIDE]
        else:
            block = jnp.zeros((TALL, WIDE), value.dtype)
        out_ref[q] = block.astype(out_ref.dtype)


def forward_kernel(place_ref, gaps_ref, source_ref, green_ref, out_ref, early, total, lag_ref):
    step, last = pl.program_id(0), pl.num_programs(0) - 1
    rows, steps, cells = source_ref.shape
    nb = green_ref.shape[0]
    height = rows * steps
    lanes = early.shape[2]

    @pl.when(step == 0)
    def _():
        for k, lag in enumerate(lags(place_ref, gaps_ref, lag_ref.shape[0])):
            lag_ref[k] = lag
        for i in range(cells // lanes):
            early[i, pl.ds(0, height), :] = jnp.zeros((height, lanes), early.dtype)
            for r in range(rows):
                piece = source_ref[r, :, i * lanes:(i + 1) * lanes].astype(jnp.float32)
                early[i, pl.ds(height + r, steps, stride=rows), :] = piece

    shifted = []
    for k in range(nb):
        start = pl.multiple_of((steps - lag_ref[step * nb + k]) * rows, rows)
        for i in range(cells // lanes):
            shifted.append(early[i, pl.ds(start, height), :].astype(jnp.bfloat16))
    shifted = jnp.concatenate(shifted, axis=1)
    stored = jnp.concatenate([green_ref[k] for k in range(nb)], axis=1)
    part = lax.dot_general(shifted, stored, (((1,), (1,)), ((), ())), preferred_element_type=jnp.float32)

    if lag_ref.shape[0] // nb > 1:
        @pl.when(step == 0)
        def _():
            total[...] = part

        @pl.when(jnp.logical_and(step > 0, step < last))
        def _():
            total[...] += part

        @pl.when(step == last)
        def _():
            cut(total[...] + part, out_ref)
    else:
        cut(part, out_ref)


def forward(place, gaps, source, green, owners, nb, wire):
    rows, steps, cells = source.shape
    blocks, sensors, _ = green.shape
    height = rows * steps
    return pl.pallas_call(
        forward_kernel,
        grid_spec=pltpu.PrefetchScalarGridSpec(
            num_scalar_prefetch=2,
            grid=(blocks // nb,),
            in_specs=[
                pl.BlockSpec((rows, steps, cells), lambda k, *_: (0, 0, 0)),
                pl.BlockSpec((nb, sensors, cells), lambda k, *_: (k, 0, 0)),
            ],
            out_specs=pl.BlockSpec((owners, TALL, WIDE), lambda k, *_: (0, 0, 0)),
            scratch_shapes=[
                pltpu.VMEM((pl.cdiv(cells, 128), 2 * height, min(cells, 128)), jnp.float32),
                pltpu.VMEM((height, sensors), jnp.float32),
                pltpu.SMEM((blocks,), jnp.int32),
            ],
        ),
        out_shape=jax.ShapeDtypeStruct((owners, TALL, WIDE), wire),
        name="forward",
    )(place, gaps, source, green)


def adjoint_kernel(place_ref, gaps_ref, weighted_ref, green_ref, out_ref, flat, late, *, rows, nb):
    height, cells = out_ref.shape
    blocks, sensors, _ = green_ref.shape
    up = height // TALL
    lag = lags(place_ref, gaps_ref, blocks)
    flat[pl.ds(height, TALL), :] = jnp.zeros((TALL, sensors), flat.dtype)
    for q in range(up * (sensors // WIDE)):
        j, a = q // up, q % up
        block = weighted_ref[q]
        late[0, pl.ds(a * TALL, TALL), pl.ds(j * WIDE, WIDE)] = block
        flat[pl.ds(a * TALL, TALL), pl.ds(j * WIDE, WIDE)] = block.astype(jnp.float32)
    late[0, pl.ds(height, height), :] = jnp.zeros((height, sensors), late.dtype)
    late[1, pl.ds(0, height), :] = flat[pl.ds(rows, height), :].astype(late.dtype)
    late[1, pl.ds(height, height), :] = jnp.zeros((height, sensors), late.dtype)
    for part in range(blocks // nb):
        windows = []
        for k in range(part * nb, part * nb + nb):
            half = lax.shift_right_logical(lag[k], 1)
            start = pl.multiple_of(half * (2 * rows), 2 * rows)
            windows.append(late[lag[k] - 2 * half, pl.ds(start, height), :])
        held = green_ref[pl.ds(part * nb, nb)].reshape(nb * sensors, cells)
        value = jnp.dot(jnp.concatenate(windows, axis=1), held, preferred_element_type=jnp.float32)
        if part == 0:
            out_ref[...] = value.astype(out_ref.dtype)
        else:
            out_ref[...] = (out_ref[...] + value).astype(out_ref.dtype)


def adjoint(place, gaps, weighted, green, rows, steps, nb):
    blocks, sensors, cells = green.shape
    height = rows * steps
    return pl.pallas_call(
        functools.partial(adjoint_kernel, rows=rows, nb=nb),
        in_specs=[SMEM, SMEM, VMEM, VMEM],
        out_specs=VMEM,
        scratch_shapes=[
            pltpu.VMEM((height + TALL, sensors), jnp.float32),
            pltpu.VMEM((2, 2 * height, sensors), jnp.bfloat16),
        ],
        out_shape=jax.ShapeDtypeStruct((height, cells), jnp.float32),
        compiler_params=LIMIT,
        name="adjoint",
    )(place, gaps, weighted, green)


def body(green, source, observed, lag_gaps, huber_level):
    rows, steps, cells = source.shape
    sensors = green.shape[1]
    depth, owners, groups = lax.axis_size("z"), lax.axis_size(PLANE), lax.axis_size("y")
    slim = TALL // depth
    up = rows * steps // TALL
    place = lax.axis_index("y")[None]

    sent = forward(place, lag_gaps, source, green, owners, 4, WIRE)
    sent = lax.all_to_all(sent, PLANE, 0, 0, tiled=True)
    plane_sum = jnp.sum(sent.astype(jnp.float32), axis=0).reshape(depth, slim, WIDE)
    summed = jnp.sum(lax.all_to_all(plane_sum, "z", 0, 0, tiled=True), axis=0)

    block = jnp.minimum(lax.axis_index(PLANE), up * (sensors // WIDE) - 1)
    column = WIDE * lax.div(block, up)
    row = TALL * lax.rem(block, up) + slim * lax.axis_index("z")
    seen = lax.dynamic_slice(observed, (lax.rem(row, rows), lax.div(row, rows), column), (slim, 1, WIDE))
    seen = seen.reshape(slim, WIDE)
    level = lax.dynamic_slice(huber_level, (column,), (WIDE,))
    threshold = 0.3 * (level.astype(jnp.float32) + 1.0)[None]
    misfit = summed - seen
    own = (misfit * threshold / jnp.maximum(jnp.abs(misfit), threshold)).astype(jnp.bfloat16)

    own = lax.all_to_all(jnp.broadcast_to(own[None], (depth, slim, WIDE)), "z", 0, 0, tiled=True)
    own = jnp.broadcast_to(own.reshape(1, TALL, WIDE), (owners, TALL, WIDE))
    weighted = lax.all_to_all(own, PLANE, 0, 0, tiled=True)

    terms = adjoint(place, lag_gaps, weighted, green, rows, steps, 4)
    terms = terms.reshape(groups, steps // groups, rows, cells)
    terms = jnp.sum(lax.all_to_all(terms, "y", 0, 0, tiled=True), axis=0)
    return terms.transpose(1, 0, 2)


def solution(mesh):
    fine = Mesh(mesh.devices.reshape(16, 4, 2, 4), ("z", "x", "c", "y"))
    cell = ("z", "x", "c")
    in_specs = (P("y", None, cell), P(None, None, cell), P(), P(), P())
    out_specs = P(None, "y", cell)
    return jax.shard_map(body, mesh=fine, in_specs=in_specs, out_specs=out_specs, check_vma=False)
```

```python
import functools
import jax
import jax.numpy as jnp
from jax import lax
from jax.experimental import pallas as pl
from jax.experimental.pallas import tpu as pltpu
from jax.sharding import Mesh, PartitionSpec as P

PLANE = ("x", "c", "y")
TALL, WIDE = 64, 128
WIRE = jnp.bfloat16
VMEM = pl.BlockSpec(memory_space=pltpu.VMEM)
SMEM = pl.BlockSpec(memory_space=pltpu.SMEM)
HBM = pl.BlockSpec(memory_space=pl.ANY)
LIMIT = pltpu.CompilerParams(vmem_limit_bytes=20 << 20)


def lags(place_ref, gaps_ref, own_count):
    before = place_ref[0] * own_count
    lag = jnp.int32(0)
    for i in range(gaps_ref.shape[0] - own_count + 1):
        lag = lag + jnp.where(i < before, gaps_ref[i], 0)
    found = [lag]
    for i in range(own_count - 1):
        lag = lag + gaps_ref[before + i]
        found.append(lag)
    return found


def forward_kernel(
    place_ref, owner_ref, gaps_ref, source_ref, green_ref, observed_ref, out_ref, seen_ref, gaps, source, green, early, total, sems, *, nb
):
    rows, steps, cells = source.shape
    blocks, sensors, _ = green.shape
    height = rows * steps
    up = height // TALL
    lanes = early.shape[2]
    parts = blocks // nb
    gaps_in = pltpu.make_async_copy(gaps_ref, gaps, sems.at[0])
    source_in = pltpu.make_async_copy(source_ref, source, sems.at[1])
    gaps_in.start()
    source_in.start()
    green_in = []
    for part in range(parts):
        at = pl.ds(part * nb, nb)
        green_in.append(pltpu.make_async_copy(green_ref.at[at], green.at[at], sems.at[2 + part]))
        green_in[-1].start()
    own = jnp.minimum(owner_ref[0], up * (sensors // WIDE) - 1)
    when = pl.ds(pl.multiple_of(lax.rem(own, up) * (TALL // rows), TALL // rows), TALL // rows)
    column = pl.ds(pl.multiple_of(lax.div(own, up) * WIDE, WIDE), WIDE)
    seen_in = pltpu.make_async_copy(observed_ref.at[:, when, column], seen_ref, sems.at[2 + parts])
    seen_in.start()
    early[:, pl.ds(0, height), :] = jnp.zeros((early.shape[0], height, lanes), early.dtype)
    gaps_in.wait()
    lag = lags(place_ref, gaps, blocks)
    source_in.wait()
    for i in range(cells // lanes):
        for r in range(rows):
            piece = source[r, :, i * lanes:(i + 1) * lanes].astype(jnp.float32)
            early[i, pl.ds(height + r, steps, stride=rows), :] = piece

    for part in range(parts):
        shifted, held = [], []
        green_in[part].wait()
        for k in range(part * nb, part * nb + nb):
            start = pl.multiple_of((steps - lag[k]) * rows, rows)
            for i in range(cells // lanes):
                shifted.append(early[i, pl.ds(start, height), :].astype(jnp.bfloat16))
            held.append(green[k])
        value = lax.dot_general(
            jnp.concatenate(shifted, axis=1), jnp.concatenate(held, axis=1),
            (((1,), (1,)), ((), ())), preferred_element_type=jnp.float32,
        )
        if part > 0:
            value = total[...] + value
        if part < parts - 1:
            total[...] = value
    for q in range(out_ref.shape[0]):
        j, a = q // up, q % up
        if j < value.shape[1] // WIDE:
            block = value[a * TALL:(a + 1) * TALL, j * WIDE:(j + 1) * WIDE]
        else:
            block = jnp.zeros((TALL, WIDE), value.dtype)
        out_ref[q] = block.astype(out_ref.dtype)
    seen_in.wait()


def forward(place, owner, gaps, source, green, observed, owners, nb, wire):
    rows, steps, cells = source.shape
    blocks, sensors, _ = green.shape
    height = rows * steps
    return pl.pallas_call(
        functools.partial(forward_kernel, nb=nb),
        in_specs=[SMEM, SMEM, HBM, HBM, HBM, HBM],
        out_specs=[VMEM, VMEM],
        scratch_shapes=[
            pltpu.SMEM(gaps.shape, gaps.dtype),
            pltpu.VMEM(source.shape, source.dtype),
            pltpu.VMEM(green.shape, green.dtype),
            pltpu.VMEM((pl.cdiv(cells, 128), 2 * height, min(cells, 128)), jnp.float32),
            pltpu.VMEM((height, sensors), jnp.float32),
            pltpu.SemaphoreType.DMA((3 + blocks // nb,)),
        ],
        out_shape=[
            jax.ShapeDtypeStruct((owners, TALL, WIDE), wire),
            jax.ShapeDtypeStruct((rows, TALL // rows, WIDE), observed.dtype),
        ],
        name="forward",
    )(place, owner, gaps, source, green, observed)


def plane_kernel(parts_ref, out_ref):
    value = parts_ref[0].astype(jnp.float32)
    for q in range(1, parts_ref.shape[0]):
        value = value + parts_ref[q].astype(jnp.float32)
    value = value.astype(out_ref.dtype)
    for p in range(out_ref.shape[0]):
        out_ref[p] = value


def plane_sum(parts, copies, wire):
    return pl.pallas_call(
        plane_kernel,
        in_specs=[VMEM],
        out_specs=VMEM,
        out_shape=jax.ShapeDtypeStruct((copies,) + parts.shape[1:], wire),
        compiler_params=LIMIT,
        name="plane_sum",
    )(parts)


def weigh_kernel(parts_ref, seen_ref, level_ref, out_ref):
    value = parts_ref[0].astype(jnp.float32)
    for p in range(1, parts_ref.shape[0]):
        value = value + parts_ref[p].astype(jnp.float32)
    threshold = 0.3 * (level_ref[...].astype(jnp.float32) + 1.0)
    misfit = value - seen_ref[...]
    weighted = (misfit * threshold / jnp.maximum(jnp.abs(misfit), threshold)).astype(out_ref.dtype)
    for q in range(out_ref.shape[0]):
        out_ref[q] = weighted


def weigh(parts, seen, level, copies):
    return pl.pallas_call(
        weigh_kernel,
        in_specs=[VMEM, VMEM, VMEM],
        out_specs=VMEM,
        out_shape=jax.ShapeDtypeStruct((copies,) + parts.shape[1:], jnp.bfloat16),
        compiler_params=LIMIT,
        name="weigh",
    )(parts, seen, level)


def adjoint_kernel(place_ref, gaps_ref, weighted_ref, green_ref, out_ref, flat, late, *, rows, nb):
    height, cells = out_ref.shape
    blocks, sensors, _ = green_ref.shape
    up = height // TALL
    lag = lags(place_ref, gaps_ref, blocks)
    flat[pl.ds(height, TALL), :] = jnp.zeros((TALL, sensors), flat.dtype)
    for q in range(up * (sensors // WIDE)):
        j, a = q // up, q % up
        block = weighted_ref[q]
        late[0, pl.ds(a * TALL, TALL), pl.ds(j * WIDE, WIDE)] = block
        flat[pl.ds(a * TALL, TALL), pl.ds(j * WIDE, WIDE)] = block.astype(jnp.float32)
    late[0, pl.ds(height, height), :] = jnp.zeros((height, sensors), late.dtype)
    late[1, pl.ds(0, height), :] = flat[pl.ds(rows, height), :].astype(late.dtype)
    late[1, pl.ds(height, height), :] = jnp.zeros((height, sensors), late.dtype)
    for part in range(blocks // nb):
        windows = []
        for k in range(part * nb, part * nb + nb):
            half = lax.shift_right_logical(lag[k], 1)
            start = pl.multiple_of(half * (2 * rows), 2 * rows)
            windows.append(late[lag[k] - 2 * half, pl.ds(start, height), :])
        held = green_ref[pl.ds(part * nb, nb)].reshape(nb * sensors, cells)
        value = jnp.dot(jnp.concatenate(windows, axis=1), held, preferred_element_type=jnp.float32)
        if part == 0:
            out_ref[...] = value.astype(out_ref.dtype)
        else:
            out_ref[...] = (out_ref[...] + value).astype(out_ref.dtype)


def adjoint(place, gaps, weighted, green, rows, steps, nb):
    blocks, sensors, cells = green.shape
    height = rows * steps
    return pl.pallas_call(
        functools.partial(adjoint_kernel, rows=rows, nb=nb),
        in_specs=[SMEM, SMEM, VMEM, VMEM],
        out_specs=VMEM,
        scratch_shapes=[
            pltpu.VMEM((height + TALL, sensors), jnp.float32),
            pltpu.VMEM((2, 2 * height, sensors), jnp.bfloat16),
        ],
        out_shape=jax.ShapeDtypeStruct((height, cells), jnp.float32),
        compiler_params=LIMIT,
        name="adjoint",
    )(place, gaps, weighted, green)


def body(green, source, observed, lag_gaps, huber_level):
    rows, steps, cells = source.shape
    sensors = green.shape[1]
    depth, owners, groups = lax.axis_size("z"), lax.axis_size(PLANE), lax.axis_size("y")
    place, owner = lax.axis_index("y")[None], lax.axis_index(PLANE)[None]

    parts, seen = forward(place, owner, lag_gaps, source, green, observed, owners, 8, WIRE)
    parts = lax.all_to_all(parts, PLANE, 0, 0, tiled=True)
    planes = lax.all_to_all(plane_sum(parts, depth, WIRE), "z", 0, 0, tiled=True)

    column = WIDE * lax.div(lax.axis_index(PLANE), rows * steps // TALL)
    level = lax.dynamic_slice(huber_level, (jnp.minimum(column, sensors - WIDE),), (WIDE,))[None]
    seen = seen.transpose(1, 0, 2).reshape(TALL, WIDE)
    weighted = weigh(planes, seen, level, owners)
    weighted = lax.all_to_all(weighted, PLANE, 0, 0, tiled=True)

    terms = adjoint(place, lag_gaps, weighted, green, rows, steps, 4)
    terms = terms.reshape(groups, steps // groups, rows, cells)
    terms = jnp.sum(lax.all_to_all(terms, "y", 0, 0, tiled=True), axis=0)
    return terms.transpose(1, 0, 2)


def solution(mesh):
    fine = Mesh(mesh.devices.reshape(16, 4, 2, 4), ("z", "x", "c", "y"))
    cell = ("z", "x", "c")
    in_specs = (P("y", None, cell), P(None, None, cell), P(), P(), P())
    out_specs = P(None, "y", cell)
    return jax.shard_map(body, mesh=fine, in_specs=in_specs, out_specs=out_specs, check_vma=False)
```

```python
import functools
import jax
import jax.numpy as jnp
from jax import lax
from jax.experimental import pallas as pl
from jax.experimental.pallas import tpu as pltpu
from jax.sharding import Mesh, PartitionSpec as P

PLANE = ("x", "c", "y")
TALL, WIDE = 64, 128
WIRE = jnp.bfloat16
VMEM = pl.BlockSpec(memory_space=pltpu.VMEM)
SMEM = pl.BlockSpec(memory_space=pltpu.SMEM)
HBM = pl.BlockSpec(memory_space=pl.ANY)
LIMIT = pltpu.CompilerParams(vmem_limit_bytes=20 << 20)


def lags(place_ref, gaps_ref, own_count):
    before = place_ref[0] * own_count
    lag = jnp.int32(0)
    for i in range(gaps_ref.shape[0] - own_count + 1):
        lag = lag + jnp.where(i < before, gaps_ref[i], 0)
    found = [lag]
    for i in range(own_count - 1):
        lag = lag + gaps_ref[before + i]
        found.append(lag)
    return found


def forward_kernel(
    place_ref, owner_ref, gaps_ref, source_ref, green_ref, observed_ref, level_ref,
    out_ref, side_ref, gaps, source, green, early, seen, level, sems
):
    rows, steps, cells = source.shape
    blocks, sensors, _ = green.shape
    height = rows * steps
    up = height // TALL
    lanes = early.shape[2]
    gaps_in = pltpu.make_async_copy(gaps_ref, gaps, sems.at[0])
    source_in = pltpu.make_async_copy(source_ref, source, sems.at[1])
    gaps_in.start()
    source_in.start()
    green_in = pltpu.make_async_copy(green_ref, green, sems.at[2])
    green_in.start()
    own = jnp.minimum(owner_ref[0], up * (sensors // WIDE) - 1)
    column = lax.div(own, up)
    when = pl.ds(pl.multiple_of(lax.rem(own, up) * (TALL // rows), TALL // rows), TALL // rows)
    where = pl.ds(pl.multiple_of(column * WIDE, WIDE), WIDE)
    seen_in = pltpu.make_async_copy(observed_ref.at[:, when, where], seen, sems.at[3])
    seen_in.start()
    level_in = pltpu.make_async_copy(level_ref, level, sems.at[4])
    level_in.start()
    early[:, pl.ds(0, height), :] = jnp.zeros((early.shape[0], height, lanes), early.dtype)
    gaps_in.wait()
    lag = lags(place_ref, gaps, blocks)
    source_in.wait()
    for i in range(cells // lanes):
        for r in range(rows):
            piece = source[r, :, i * lanes:(i + 1) * lanes].astype(jnp.float32)
            early[i, pl.ds(height + r, steps, stride=rows), :] = piece

    shifted = []
    for k in range(blocks):
        start = pl.multiple_of((steps - lag[k]) * rows, rows)
        for i in range(cells // lanes):
            shifted.append(early[i, pl.ds(start, height), :].astype(jnp.bfloat16))
    green_in.wait()
    value = lax.dot_general(
        jnp.concatenate(shifted, axis=1), jnp.concatenate([green[k] for k in range(blocks)], axis=1),
        (((1,), (1,)), ((), ())), preferred_element_type=jnp.float32,
    )
    for q in range(out_ref.shape[0]):
        j, a = q // up, q % up
        if j < value.shape[1] // WIDE:
            block = value[a * TALL:(a + 1) * TALL, j * WIDE:(j + 1) * WIDE]
        else:
            block = jnp.zeros((TALL, WIDE), value.dtype)
        out_ref[q] = block.astype(out_ref.dtype)
    seen_in.wait()
    level_in.wait()
    tall = TALL // rows
    for r in range(rows):
        side_ref[pl.ds(r, tall, stride=rows), :] = seen[r]
    threshold = 0.3 * (level[pl.ds(column, 1), :].astype(jnp.float32) + 1.0)
    side_ref[pl.ds(TALL, 8), :] = jnp.broadcast_to(threshold, (8, WIDE))


def forward(place, owner, gaps, source, green, observed, level, owners, wire):
    rows, steps, cells = source.shape
    blocks, sensors, _ = green.shape
    height = rows * steps
    return pl.pallas_call(
        forward_kernel,
        in_specs=[SMEM, SMEM, HBM, HBM, HBM, HBM, HBM],
        out_specs=[VMEM, VMEM],
        scratch_shapes=[
            pltpu.SMEM(gaps.shape, gaps.dtype),
            pltpu.VMEM(source.shape, source.dtype),
            pltpu.VMEM(green.shape, green.dtype),
            pltpu.VMEM((pl.cdiv(cells, 128), 2 * height, min(cells, 128)), jnp.float32),
            pltpu.VMEM((rows, TALL // rows, WIDE), observed.dtype),
            pltpu.VMEM(level.shape, level.dtype),
            pltpu.SemaphoreType.DMA((5,)),
        ],
        out_shape=[
            jax.ShapeDtypeStruct((owners, TALL, WIDE), wire),
            jax.ShapeDtypeStruct((TALL + 8, WIDE), observed.dtype),
        ],
        name="forward",
    )(place, owner, gaps, source, green, observed, level)


def plane_kernel(parts_ref, out_ref):
    value = parts_ref[0].astype(jnp.float32)
    for q in range(1, parts_ref.shape[0]):
        value = value + parts_ref[q].astype(jnp.float32)
    value = value.astype(out_ref.dtype)
    for p in range(out_ref.shape[0]):
        out_ref[p] = value


def plane_sum(parts, copies, wire):
    return pl.pallas_call(
        plane_kernel,
        in_specs=[VMEM],
        out_specs=VMEM,
        out_shape=jax.ShapeDtypeStruct((copies,) + parts.shape[1:], wire),
        compiler_params=LIMIT,
        name="plane_sum",
    )(parts)


def weigh_kernel(parts_ref, side_ref, out_ref, side, sem):
    side_in = pltpu.make_async_copy(side_ref, side, sem)
    side_in.start()
    value = parts_ref[0].astype(jnp.float32)
    for p in range(1, parts_ref.shape[0]):
        value = value + parts_ref[p].astype(jnp.float32)
    side_in.wait()
    tall = parts_ref.shape[1]
    misfit = value - side[pl.ds(0, tall), :]
    threshold = side[pl.ds(tall, 1), :]
    weighted = (misfit * threshold / jnp.maximum(jnp.abs(misfit), threshold)).astype(out_ref.dtype)
    for q in range(out_ref.shape[0]):
        out_ref[q] = weighted


def weigh(parts, side, copies):
    return pl.pallas_call(
        weigh_kernel,
        in_specs=[VMEM, HBM],
        out_specs=VMEM,
        scratch_shapes=[pltpu.VMEM(side.shape, side.dtype), pltpu.SemaphoreType.DMA],
        out_shape=jax.ShapeDtypeStruct((copies,) + parts.shape[1:], jnp.bfloat16),
        compiler_params=LIMIT,
        name="weigh",
    )(parts, side)


def adjoint_kernel(place_ref, gaps_ref, weighted_ref, green_ref, out_ref, flat, late, *, rows, nb):
    height, cells = out_ref.shape
    blocks, sensors, _ = green_ref.shape
    up = height // TALL
    lag = lags(place_ref, gaps_ref, blocks)
    flat[pl.ds(height, TALL), :] = jnp.zeros((TALL, sensors), flat.dtype)
    for q in range(up * (sensors // WIDE)):
        j, a = q // up, q % up
        block = weighted_ref[q]
        late[0, pl.ds(a * TALL, TALL), pl.ds(j * WIDE, WIDE)] = block
        flat[pl.ds(a * TALL, TALL), pl.ds(j * WIDE, WIDE)] = block.astype(jnp.float32)
    late[0, pl.ds(height, height), :] = jnp.zeros((height, sensors), late.dtype)
    late[1, pl.ds(0, height), :] = flat[pl.ds(rows, height), :].astype(late.dtype)
    late[1, pl.ds(height, height), :] = jnp.zeros((height, sensors), late.dtype)
    for part in range(blocks // nb):
        windows = []
        for k in range(part * nb, part * nb + nb):
            half = lax.shift_right_logical(lag[k], 1)
            start = pl.multiple_of(half * (2 * rows), 2 * rows)
            windows.append(late[lag[k] - 2 * half, pl.ds(start, height), :])
        held = green_ref[pl.ds(part * nb, nb)].reshape(nb * sensors, cells)
        value = jnp.dot(jnp.concatenate(windows, axis=1), held, preferred_element_type=jnp.float32)
        if part == 0:
            out_ref[...] = value.astype(out_ref.dtype)
        else:
            out_ref[...] = (out_ref[...] + value).astype(out_ref.dtype)


def adjoint(place, gaps, weighted, green, rows, steps, nb):
    blocks, sensors, cells = green.shape
    height = rows * steps
    return pl.pallas_call(
        functools.partial(adjoint_kernel, rows=rows, nb=nb),
        in_specs=[SMEM, SMEM, VMEM, VMEM],
        out_specs=VMEM,
        scratch_shapes=[
            pltpu.VMEM((height + TALL, sensors), jnp.float32),
            pltpu.VMEM((2, 2 * height, sensors), jnp.bfloat16),
        ],
        out_shape=jax.ShapeDtypeStruct((height, cells), jnp.float32),
        compiler_params=LIMIT,
        name="adjoint",
    )(place, gaps, weighted, green)


def body(green, source, observed, lag_gaps, huber_level):
    rows, steps, cells = source.shape
    sensors = green.shape[1]
    depth, owners, groups = lax.axis_size("z"), lax.axis_size(PLANE), lax.axis_size("y")
    place, owner = lax.axis_index("y")[None], lax.axis_index(PLANE)[None]

    level = huber_level.reshape(sensors // WIDE, WIDE)
    parts, side = forward(place, owner, lag_gaps, source, green, observed, level, owners, WIRE)
    parts = lax.all_to_all(parts, PLANE, 0, 0, tiled=True)
    planes = lax.all_to_all(plane_sum(parts, depth, WIRE), "z", 0, 0, tiled=True)

    weighted = weigh(planes, side, owners)
    weighted = lax.all_to_all(weighted, PLANE, 0, 0, tiled=True)

    terms = adjoint(place, lag_gaps, weighted, green, rows, steps, 4)
    terms = terms.reshape(groups, steps // groups, rows, cells)
    terms = jnp.sum(lax.all_to_all(terms, "y", 0, 0, tiled=True), axis=0)
    return terms.transpose(1, 0, 2)


def solution(mesh):
    fine = Mesh(mesh.devices.reshape(16, 4, 2, 4), ("z", "x", "c", "y"))
    cell = ("z", "x", "c")
    in_specs = (P("y", None, cell), P(None, None, cell), P(), P(), P())
    out_specs = P(None, "y", cell)
    return jax.shard_map(body, mesh=fine, in_specs=in_specs, out_specs=out_specs, check_vma=False)
```

```python
import functools
import jax
import jax.numpy as jnp
from jax import lax
from jax.experimental import pallas as pl
from jax.experimental.pallas import tpu as pltpu
from jax.sharding import Mesh, PartitionSpec as P

PLANE = ("x", "c", "y")
TALL, WIDE = 64, 128
WIRE = jnp.bfloat16
VMEM = pl.BlockSpec(memory_space=pltpu.VMEM)
SMEM = pl.BlockSpec(memory_space=pltpu.SMEM)
HBM = pl.BlockSpec(memory_space=pl.ANY)
LIMIT = pltpu.CompilerParams(vmem_limit_bytes=20 << 20)


def lags(place_ref, gaps_ref, own_count):
    before = place_ref[0] * own_count
    lag = jnp.int32(0)
    for i in range(gaps_ref.shape[0] - own_count + 1):
        lag = lag + jnp.where(i < before, gaps_ref[i], 0)
    found = [lag]
    for i in range(own_count - 1):
        lag = lag + gaps_ref[before + i]
        found.append(lag)
    return found


def forward_kernel(
    place_ref, owner_ref, gaps_ref, source_ref, green_ref, observed_ref, level_ref,
    out_ref, side_ref, gaps, source, green, early, seen, level, sems
):
    rows, steps, cells = source.shape
    blocks, sensors, _ = green.shape
    height = rows * steps
    up = height // TALL
    lanes = early.shape[2]
    gaps_in = pltpu.make_async_copy(gaps_ref, gaps, sems.at[0])
    source_in = pltpu.make_async_copy(source_ref, source, sems.at[1])
    gaps_in.start()
    source_in.start()
    green_in = pltpu.make_async_copy(green_ref, green, sems.at[2])
    green_in.start()
    own = jnp.minimum(owner_ref[0], up * (sensors // WIDE) - 1)
    column = lax.div(own, up)
    when = pl.ds(pl.multiple_of(lax.rem(own, up) * (TALL // rows), TALL // rows), TALL // rows)
    where = pl.ds(pl.multiple_of(column * WIDE, WIDE), WIDE)
    seen_in = pltpu.make_async_copy(observed_ref.at[:, when, where], seen, sems.at[3])
    seen_in.start()
    level_in = pltpu.make_async_copy(level_ref, level, sems.at[4])
    level_in.start()
    early[:, pl.ds(0, height), :] = jnp.zeros((early.shape[0], height, lanes), early.dtype)
    gaps_in.wait()
    lag = lags(place_ref, gaps, blocks)
    source_in.wait()
    for i in range(cells // lanes):
        for r in range(rows):
            piece = source[r, :, i * lanes:(i + 1) * lanes].astype(jnp.float32)
            early[i, pl.ds(height + r, steps, stride=rows), :] = piece

    shifted = []
    for k in range(blocks):
        start = pl.multiple_of((steps - lag[k]) * rows, rows)
        for i in range(cells // lanes):
            shifted.append(early[i, pl.ds(start, height), :].astype(jnp.bfloat16))
    green_in.wait()
    value = lax.dot_general(
        jnp.concatenate(shifted, axis=1), jnp.concatenate([green[k] for k in range(blocks)], axis=1),
        (((1,), (1,)), ((), ())), preferred_element_type=jnp.float32,
    )
    for q in range(out_ref.shape[0]):
        j, a = q // up, q % up
        if j < value.shape[1] // WIDE:
            block = value[a * TALL:(a + 1) * TALL, j * WIDE:(j + 1) * WIDE]
        else:
            block = jnp.zeros((TALL, WIDE), value.dtype)
        out_ref[q] = block.astype(out_ref.dtype)
    seen_in.wait()
    level_in.wait()
    tall = TALL // rows
    for r in range(rows):
        side_ref[pl.ds(r, tall, stride=rows), :] = seen[r]
    threshold = 0.3 * (level[pl.ds(column, 1), :].astype(jnp.float32) + 1.0)
    side_ref[pl.ds(TALL, 8), :] = jnp.broadcast_to(threshold, (8, WIDE))


def forward(place, owner, gaps, source, green, observed, level, owners, wire):
    rows, steps, cells = source.shape
    blocks, sensors, _ = green.shape
    height = rows * steps
    return pl.pallas_call(
        forward_kernel,
        in_specs=[SMEM, SMEM, HBM, HBM, HBM, HBM, HBM],
        out_specs=[VMEM, VMEM],
        scratch_shapes=[
            pltpu.SMEM(gaps.shape, gaps.dtype),
            pltpu.VMEM(source.shape, source.dtype),
            pltpu.VMEM(green.shape, green.dtype),
            pltpu.VMEM((pl.cdiv(cells, 128), 2 * height, min(cells, 128)), jnp.float32),
            pltpu.VMEM((rows, TALL // rows, WIDE), observed.dtype),
            pltpu.VMEM(level.shape, level.dtype),
            pltpu.SemaphoreType.DMA((5,)),
        ],
        out_shape=[
            pltpu.VMEM((owners, TALL, WIDE), wire),
            pltpu.VMEM((TALL + 8, WIDE), observed.dtype),
        ],
        name="forward",
    )(place, owner, gaps, source, green, observed, level)


def plane_kernel(parts_ref, out_ref):
    value = parts_ref[0].astype(jnp.float32)
    for q in range(1, parts_ref.shape[0]):
        value = value + parts_ref[q].astype(jnp.float32)
    value = value.astype(out_ref.dtype)
    for p in range(out_ref.shape[0]):
        out_ref[p] = value


def plane_sum(parts, copies, wire):
    return pl.pallas_call(
        plane_kernel,
        in_specs=[VMEM],
        out_specs=VMEM,
        out_shape=jax.ShapeDtypeStruct((copies,) + parts.shape[1:], wire),
        compiler_params=LIMIT,
        name="plane_sum",
    )(parts)


def weigh_kernel(parts_ref, side_ref, out_ref):
    value = parts_ref[0].astype(jnp.float32)
    for p in range(1, parts_ref.shape[0]):
        value = value + parts_ref[p].astype(jnp.float32)
    tall = parts_ref.shape[1]
    misfit = value - side_ref[pl.ds(0, tall), :]
    threshold = side_ref[pl.ds(tall, 1), :]
    weighted = (misfit * threshold / jnp.maximum(jnp.abs(misfit), threshold)).astype(out_ref.dtype)
    for q in range(out_ref.shape[0]):
        out_ref[q] = weighted


def weigh(parts, side, copies):
    return pl.pallas_call(
        weigh_kernel,
        in_specs=[VMEM, VMEM],
        out_specs=VMEM,
        out_shape=jax.ShapeDtypeStruct((copies,) + parts.shape[1:], jnp.bfloat16),
        compiler_params=LIMIT,
        name="weigh",
    )(parts, side)


def fold_kernel(parts_ref, out_ref):
    value = parts_ref[0]
    for y in range(1, parts_ref.shape[0]):
        value = value + parts_ref[y]
    out_ref[...] = value


def fold(parts):
    return pl.pallas_call(
        fold_kernel,
        in_specs=[VMEM],
        out_specs=VMEM,
        out_shape=jax.ShapeDtypeStruct(parts.shape[1:], parts.dtype),
        compiler_params=LIMIT,
        name="fold",
    )(parts)


def adjoint_kernel(place_ref, gaps_ref, weighted_ref, green_ref, out_ref, flat, late, *, rows, nb):
    height, cells = out_ref.shape
    blocks, sensors, _ = green_ref.shape
    up = height // TALL
    lag = lags(place_ref, gaps_ref, blocks)
    flat[pl.ds(height, TALL), :] = jnp.zeros((TALL, sensors), flat.dtype)
    for q in range(up * (sensors // WIDE)):
        j, a = q // up, q % up
        block = weighted_ref[q]
        late[0, pl.ds(a * TALL, TALL), pl.ds(j * WIDE, WIDE)] = block
        flat[pl.ds(a * TALL, TALL), pl.ds(j * WIDE, WIDE)] = block.astype(jnp.float32)
    late[0, pl.ds(height, height), :] = jnp.zeros((height, sensors), late.dtype)
    late[1, pl.ds(0, height), :] = flat[pl.ds(rows, height), :].astype(late.dtype)
    late[1, pl.ds(height, height), :] = jnp.zeros((height, sensors), late.dtype)
    for part in range(blocks // nb):
        windows = []
        for k in range(part * nb, part * nb + nb):
            half = lax.shift_right_logical(lag[k], 1)
            start = pl.multiple_of(half * (2 * rows), 2 * rows)
            windows.append(late[lag[k] - 2 * half, pl.ds(start, height), :])
        held = green_ref[pl.ds(part * nb, nb)].reshape(nb * sensors, cells)
        value = jnp.dot(jnp.concatenate(windows, axis=1), held, preferred_element_type=jnp.float32)
        if part == 0:
            out_ref[...] = value.astype(out_ref.dtype)
        else:
            out_ref[...] = (out_ref[...] + value).astype(out_ref.dtype)


def adjoint(place, gaps, weighted, green, rows, steps, nb):
    blocks, sensors, cells = green.shape
    height = rows * steps
    return pl.pallas_call(
        functools.partial(adjoint_kernel, rows=rows, nb=nb),
        in_specs=[SMEM, SMEM, VMEM, VMEM],
        out_specs=VMEM,
        scratch_shapes=[
            pltpu.VMEM((height + TALL, sensors), jnp.float32),
            pltpu.VMEM((2, 2 * height, sensors), jnp.bfloat16),
        ],
        out_shape=jax.ShapeDtypeStruct((height, cells), jnp.float32),
        compiler_params=LIMIT,
        name="adjoint",
    )(place, gaps, weighted, green)


def body(green, source, observed, lag_gaps, huber_level):
    rows, steps, cells = source.shape
    sensors = green.shape[1]
    depth, owners, groups = lax.axis_size("z"), lax.axis_size(PLANE), lax.axis_size("y")
    place, owner = lax.axis_index("y")[None], lax.axis_index(PLANE)[None]

    level = huber_level.reshape(sensors // WIDE, WIDE)
    parts, side = forward(place, owner, lag_gaps, source, green, observed, level, owners, WIRE)
    parts = lax.all_to_all(parts, PLANE, 0, 0, tiled=True)
    planes = lax.all_to_all(plane_sum(parts, depth, WIRE), "z", 0, 0, tiled=True)

    weighted = weigh(planes, side, owners)
    weighted = lax.all_to_all(weighted, PLANE, 0, 0, tiled=True)

    terms = adjoint(place, lag_gaps, weighted, green, rows, steps, 4)
    terms = terms.reshape(groups, steps // groups, rows, cells)
    terms = fold(lax.all_to_all(terms, "y", 0, 0, tiled=True))
    return terms.transpose(1, 0, 2)


def solution(mesh):
    fine = Mesh(mesh.devices.reshape(16, 4, 2, 4), ("z", "x", "c", "y"))
    cell = ("z", "x", "c")
    in_specs = (P("y", None, cell), P(None, None, cell), P(), P(), P())
    out_specs = P(None, "y", cell)
    return jax.shard_map(body, mesh=fine, in_specs=in_specs, out_specs=out_specs, check_vma=False)
```

```python
import functools
import jax
import jax.numpy as jnp
from jax import lax
from jax.experimental import pallas as pl
from jax.experimental.pallas import tpu as pltpu
from jax.sharding import Mesh, PartitionSpec as P

PLANE = ("x", "c", "y")
TALL, WIDE = 64, 128
WIRE = jnp.float32
VMEM = pl.BlockSpec(memory_space=pltpu.VMEM)
SMEM = pl.BlockSpec(memory_space=pltpu.SMEM)
HBM = pl.BlockSpec(memory_space=pl.ANY)
LIMIT = pltpu.CompilerParams(vmem_limit_bytes=20 << 20)


def lags(place_ref, gaps_ref, own_count):
    before = place_ref[0] * own_count
    lag = jnp.int32(0)
    for i in range(gaps_ref.shape[0] - own_count + 1):
        lag = lag + jnp.where(i < before, gaps_ref[i], 0)
    found = [lag]
    for i in range(own_count - 1):
        lag = lag + gaps_ref[before + i]
        found.append(lag)
    return found


def forward_kernel(
    place_ref, owner_ref, gaps_ref, source_ref, green_ref, observed_ref, level_ref,
    out_ref, side_ref, gaps, source, green, early, seen, level, sems
):
    rows, steps, cells = source.shape
    blocks, sensors, _ = green.shape
    height = rows * steps
    up = height // TALL
    lanes = early.shape[2]
    gaps_in = pltpu.make_async_copy(gaps_ref, gaps, sems.at[0])
    source_in = pltpu.make_async_copy(source_ref, source, sems.at[1])
    gaps_in.start()
    source_in.start()
    green_in = pltpu.make_async_copy(green_ref, green, sems.at[2])
    green_in.start()
    own = jnp.minimum(owner_ref[0], up * (sensors // WIDE) - 1)
    column = lax.div(own, up)
    when = pl.ds(pl.multiple_of(lax.rem(own, up) * (TALL // rows), TALL // rows), TALL // rows)
    where = pl.ds(pl.multiple_of(column * WIDE, WIDE), WIDE)
    seen_in = pltpu.make_async_copy(observed_ref.at[:, when, where], seen, sems.at[3])
    seen_in.start()
    level_in = pltpu.make_async_copy(level_ref, level, sems.at[4])
    level_in.start()
    early[:, pl.ds(0, height), :] = jnp.zeros((early.shape[0], height, lanes), early.dtype)
    gaps_in.wait()
    lag = lags(place_ref, gaps, blocks)
    source_in.wait()
    for i in range(cells // lanes):
        for r in range(rows):
            piece = source[r, :, i * lanes:(i + 1) * lanes].astype(jnp.float32)
            early[i, pl.ds(height + r, steps, stride=rows), :] = piece

    shifted = []
    for k in range(blocks):
        start = pl.multiple_of((steps - lag[k]) * rows, rows)
        for i in range(cells // lanes):
            shifted.append(early[i, pl.ds(start, height), :].astype(jnp.bfloat16))
    green_in.wait()
    value = lax.dot_general(
        jnp.concatenate(shifted, axis=1), jnp.concatenate([green[k] for k in range(blocks)], axis=1),
        (((1,), (1,)), ((), ())), preferred_element_type=jnp.float32,
    )
    for q in range(out_ref.shape[0]):
        j, a = q // up, q % up
        if j < value.shape[1] // WIDE:
            block = value[a * TALL:(a + 1) * TALL, j * WIDE:(j + 1) * WIDE]
        else:
            block = jnp.zeros((TALL, WIDE), value.dtype)
        out_ref[q] = block.astype(out_ref.dtype)
    seen_in.wait()
    level_in.wait()
    tall = TALL // rows
    for r in range(rows):
        side_ref[pl.ds(r, tall, stride=rows), :] = seen[r]
    threshold = 0.3 * (level[pl.ds(column, 1), :].astype(jnp.float32) + 1.0)
    side_ref[pl.ds(TALL, 8), :] = jnp.broadcast_to(threshold, (8, WIDE))


def forward(place, owner, gaps, source, green, observed, level, owners, wire):
    rows, steps, cells = source.shape
    blocks, sensors, _ = green.shape
    height = rows * steps
    return pl.pallas_call(
        forward_kernel,
        in_specs=[SMEM, SMEM, HBM, HBM, HBM, HBM, HBM],
        out_specs=[VMEM, VMEM],
        scratch_shapes=[
            pltpu.SMEM(gaps.shape, gaps.dtype),
            pltpu.VMEM(source.shape, source.dtype),
            pltpu.VMEM(green.shape, green.dtype),
            pltpu.VMEM((pl.cdiv(cells, 128), 2 * height, min(cells, 128)), jnp.float32),
            pltpu.VMEM((rows, TALL // rows, WIDE), observed.dtype),
            pltpu.VMEM(level.shape, level.dtype),
            pltpu.SemaphoreType.DMA((5,)),
        ],
        out_shape=[
            pltpu.VMEM((owners, TALL, WIDE), wire),
            pltpu.VMEM((TALL + 8, WIDE), observed.dtype),
        ],
        name="forward",
    )(place, owner, gaps, source, green, observed, level)


def plane_kernel(parts_ref, out_ref):
    value = parts_ref[0].astype(jnp.float32)
    for q in range(1, parts_ref.shape[0]):
        value = value + parts_ref[q].astype(jnp.float32)
    value = value.astype(out_ref.dtype)
    for p in range(out_ref.shape[0]):
        out_ref[p] = value


def plane_sum(parts, copies, wire):
    return pl.pallas_call(
        plane_kernel,
        in_specs=[VMEM],
        out_specs=VMEM,
        out_shape=jax.ShapeDtypeStruct((copies,) + parts.shape[1:], wire),
        compiler_params=LIMIT,
        name="plane_sum",
    )(parts)


def weigh_kernel(parts_ref, side_ref, out_ref):
    value = parts_ref[0].astype(jnp.float32)
    for p in range(1, parts_ref.shape[0]):
        value = value + parts_ref[p].astype(jnp.float32)
    tall = parts_ref.shape[1]
    misfit = value - side_ref[pl.ds(0, tall), :]
    threshold = side_ref[pl.ds(tall, 1), :]
    weighted = (misfit * threshold / jnp.maximum(jnp.abs(misfit), threshold)).astype(out_ref.dtype)
    for q in range(out_ref.shape[0]):
        out_ref[q] = weighted


def weigh(parts, side, copies):
    return pl.pallas_call(
        weigh_kernel,
        in_specs=[VMEM, VMEM],
        out_specs=VMEM,
        out_shape=jax.ShapeDtypeStruct((copies,) + parts.shape[1:], jnp.bfloat16),
        compiler_params=LIMIT,
        name="weigh",
    )(parts, side)


def fold_kernel(parts_ref, out_ref):
    value = parts_ref[0]
    for y in range(1, parts_ref.shape[0]):
        value = value + parts_ref[y]
    out_ref[...] = value


def fold(parts):
    return pl.pallas_call(
        fold_kernel,
        in_specs=[VMEM],
        out_specs=VMEM,
        out_shape=jax.ShapeDtypeStruct(parts.shape[1:], parts.dtype),
        compiler_params=LIMIT,
        name="fold",
    )(parts)


def adjoint_kernel(place_ref, gaps_ref, weighted_ref, green_ref, out_ref, flat, late, *, rows, nb):
    height, cells = out_ref.shape
    blocks, sensors, _ = green_ref.shape
    up = height // TALL
    lag = lags(place_ref, gaps_ref, blocks)
    flat[pl.ds(height, TALL), :] = jnp.zeros((TALL, sensors), flat.dtype)
    for q in range(up * (sensors // WIDE)):
        j, a = q // up, q % up
        block = weighted_ref[q]
        late[0, pl.ds(a * TALL, TALL), pl.ds(j * WIDE, WIDE)] = block
        flat[pl.ds(a * TALL, TALL), pl.ds(j * WIDE, WIDE)] = block.astype(jnp.float32)
    late[0, pl.ds(height, height), :] = jnp.zeros((height, sensors), late.dtype)
    late[1, pl.ds(0, height), :] = flat[pl.ds(rows, height), :].astype(late.dtype)
    late[1, pl.ds(height, height), :] = jnp.zeros((height, sensors), late.dtype)
    for part in range(blocks // nb):
        windows = []
        for k in range(part * nb, part * nb + nb):
            half = lax.shift_right_logical(lag[k], 1)
            start = pl.multiple_of(half * (2 * rows), 2 * rows)
            windows.append(late[lag[k] - 2 * half, pl.ds(start, height), :])
        held = green_ref[pl.ds(part * nb, nb)].reshape(nb * sensors, cells)
        value = jnp.dot(jnp.concatenate(windows, axis=1), held, preferred_element_type=jnp.float32)
        if part == 0:
            out_ref[...] = value.astype(out_ref.dtype)
        else:
            out_ref[...] = (out_ref[...] + value).astype(out_ref.dtype)


def adjoint(place, gaps, weighted, green, rows, steps, nb):
    blocks, sensors, cells = green.shape
    height = rows * steps
    return pl.pallas_call(
        functools.partial(adjoint_kernel, rows=rows, nb=nb),
        in_specs=[SMEM, SMEM, VMEM, VMEM],
        out_specs=VMEM,
        scratch_shapes=[
            pltpu.VMEM((height + TALL, sensors), jnp.float32),
            pltpu.VMEM((2, 2 * height, sensors), jnp.bfloat16),
        ],
        out_shape=jax.ShapeDtypeStruct((height, cells), jnp.float32),
        compiler_params=LIMIT,
        name="adjoint",
    )(place, gaps, weighted, green)


def body(green, source, observed, lag_gaps, huber_level):
    rows, steps, cells = source.shape
    sensors = green.shape[1]
    depth, owners, groups = lax.axis_size("z"), lax.axis_size(PLANE), lax.axis_size("y")
    place, owner = lax.axis_index("y")[None], lax.axis_index(PLANE)[None]

    level = huber_level.reshape(sensors // WIDE, WIDE)
    parts, side = forward(place, owner, lag_gaps, source, green, observed, level, owners, WIRE)
    parts = lax.all_to_all(parts, PLANE, 0, 0, tiled=True)
    planes = lax.all_to_all(plane_sum(parts, depth, WIRE), "z", 0, 0, tiled=True)

    weighted = weigh(planes, side, owners)
    weighted = lax.all_to_all(weighted, PLANE, 0, 0, tiled=True)

    terms = adjoint(place, lag_gaps, weighted, green, rows, steps, 4)
    terms = terms.reshape(groups, steps // groups, rows, cells)
    terms = fold(lax.all_to_all(terms, "y", 0, 0, tiled=True))
    return terms.transpose(1, 0, 2)


def solution(mesh):
    fine = Mesh(mesh.devices.reshape(16, 4, 2, 4), ("z", "x", "c", "y"))
    cell = ("z", "x", "c")
    in_specs = (P("y", None, cell), P(None, None, cell), P(), P(), P())
    out_specs = P(None, "y", cell)
    return jax.shard_map(body, mesh=fine, in_specs=in_specs, out_specs=out_specs, check_vma=False)
```

```python
import functools
import jax
import jax.numpy as jnp
from jax import lax
from jax.experimental import pallas as pl
from jax.experimental.pallas import tpu as pltpu
from jax.sharding import Mesh, PartitionSpec as P

PLANE = ("x", "c", "y")
TALL, WIDE = 64, 128
WIRE = jnp.bfloat16
VMEM = pl.BlockSpec(memory_space=pltpu.VMEM)
SMEM = pl.BlockSpec(memory_space=pltpu.SMEM)
HBM = pl.BlockSpec(memory_space=pl.ANY)
LIMIT = pltpu.CompilerParams(vmem_limit_bytes=20 << 20)


def lags(place_ref, gaps_ref, own_count):
    before = place_ref[0] * own_count
    lag = jnp.int32(0)
    for i in range(gaps_ref.shape[0] - own_count + 1):
        lag = lag + jnp.where(i < before, gaps_ref[i], 0)
    found = [lag]
    for i in range(own_count - 1):
        lag = lag + gaps_ref[before + i]
        found.append(lag)
    return found


def forward_kernel(
    place_ref, owner_ref, gaps_ref, source_ref, green_ref, observed_ref, level_ref,
    out_ref, side_ref, gaps, source, green, early, seen, level, sems
):
    rows, steps, cells = source.shape
    blocks, sensors, _ = green.shape
    height = rows * steps
    up = height // TALL
    lanes = early.shape[2]
    gaps_in = pltpu.make_async_copy(gaps_ref, gaps, sems.at[0])
    source_in = pltpu.make_async_copy(source_ref, source, sems.at[1])
    gaps_in.start()
    source_in.start()
    green_in = pltpu.make_async_copy(green_ref, green, sems.at[2])
    green_in.start()
    own = jnp.minimum(owner_ref[0], up * (sensors // WIDE) - 1)
    column = lax.div(own, up)
    when = pl.ds(pl.multiple_of(lax.rem(own, up) * (TALL // rows), TALL // rows), TALL // rows)
    where = pl.ds(pl.multiple_of(column * WIDE, WIDE), WIDE)
    seen_in = pltpu.make_async_copy(observed_ref.at[:, when, where], seen, sems.at[3])
    seen_in.start()
    level_in = pltpu.make_async_copy(level_ref, level, sems.at[4])
    level_in.start()
    early[:, pl.ds(0, height), :] = jnp.zeros((early.shape[0], height, lanes), early.dtype)
    gaps_in.wait()
    lag = lags(place_ref, gaps, blocks)
    source_in.wait()
    for i in range(cells // lanes):
        for r in range(rows):
            piece = source[r, :, i * lanes:(i + 1) * lanes].astype(jnp.float32)
            early[i, pl.ds(height + r, steps, stride=rows), :] = piece

    shifted = []
    for k in range(blocks):
        start = pl.multiple_of((steps - lag[k]) * rows, rows)
        for i in range(cells // lanes):
            shifted.append(early[i, pl.ds(start, height), :].astype(jnp.bfloat16))
    green_in.wait()
    value = lax.dot_general(
        jnp.concatenate(shifted, axis=1), jnp.concatenate([green[k] for k in range(blocks)], axis=1),
        (((1,), (1,)), ((), ())), preferred_element_type=jnp.float32,
    )
    for q in range(out_ref.shape[0]):
        j, a = q // up, q % up
        if j < value.shape[1] // WIDE:
            block = value[a * TALL:(a + 1) * TALL, j * WIDE:(j + 1) * WIDE]
        else:
            block = jnp.zeros((TALL, WIDE), value.dtype)
        out_ref[q] = block.astype(out_ref.dtype)
    seen_in.wait()
    level_in.wait()
    tall = TALL // rows
    for r in range(rows):
        side_ref[pl.ds(r, tall, stride=rows), :] = seen[r]
    threshold = 0.3 * (level[pl.ds(column, 1), :].astype(jnp.float32) + 1.0)
    side_ref[pl.ds(TALL, 8), :] = jnp.broadcast_to(threshold, (8, WIDE))


def forward(place, owner, gaps, source, green, observed, level, owners, wire):
    rows, steps, cells = source.shape
    blocks, sensors, _ = green.shape
    height = rows * steps
    return pl.pallas_call(
        forward_kernel,
        in_specs=[SMEM, SMEM, HBM, HBM, HBM, HBM, HBM],
        out_specs=[VMEM, VMEM],
        scratch_shapes=[
            pltpu.SMEM(gaps.shape, gaps.dtype),
            pltpu.VMEM(source.shape, source.dtype),
            pltpu.VMEM(green.shape, green.dtype),
            pltpu.VMEM((pl.cdiv(cells, 128), 2 * height, min(cells, 128)), jnp.float32),
            pltpu.VMEM((rows, TALL // rows, WIDE), observed.dtype),
            pltpu.VMEM(level.shape, level.dtype),
            pltpu.SemaphoreType.DMA((5,)),
        ],
        out_shape=[
            pltpu.VMEM((owners, TALL, WIDE), wire),
            pltpu.VMEM((TALL + 8, WIDE), observed.dtype),
        ],
        name="forward",
    )(place, owner, gaps, source, green, observed, level)


def plane_kernel(parts_ref, out_ref):
    value = parts_ref[0].astype(jnp.float32)
    for q in range(1, parts_ref.shape[0]):
        value = value + parts_ref[q].astype(jnp.float32)
    value = value.astype(out_ref.dtype)
    for p in range(out_ref.shape[0]):
        out_ref[p] = value


def plane_sum(parts, copies, wire):
    return pl.pallas_call(
        plane_kernel,
        in_specs=[VMEM],
        out_specs=VMEM,
        out_shape=jax.ShapeDtypeStruct((copies,) + parts.shape[1:], wire),
        compiler_params=LIMIT,
        name="plane_sum",
    )(parts)


def weigh_kernel(parts_ref, side_ref, out_ref):
    value = parts_ref[0].astype(jnp.float32)
    for p in range(1, parts_ref.shape[0]):
        value = value + parts_ref[p].astype(jnp.float32)
    tall = parts_ref.shape[1]
    misfit = value - side_ref[pl.ds(0, tall), :]
    threshold = side_ref[pl.ds(tall, 1), :]
    weighted = (misfit * threshold / jnp.maximum(jnp.abs(misfit), threshold)).astype(out_ref.dtype)
    for q in range(out_ref.shape[0]):
        out_ref[q] = weighted


def weigh(parts, side, copies):
    return pl.pallas_call(
        weigh_kernel,
        in_specs=[VMEM, VMEM],
        out_specs=VMEM,
        out_shape=jax.ShapeDtypeStruct((copies,) + parts.shape[1:], jnp.bfloat16),
        compiler_params=LIMIT,
        name="weigh",
    )(parts, side)


def fold_kernel(parts_ref, out_ref):
    value = parts_ref[0]
    for y in range(1, parts_ref.shape[0]):
        value = value + parts_ref[y]
    out_ref[...] = value


def fold(parts):
    return pl.pallas_call(
        fold_kernel,
        in_specs=[VMEM],
        out_specs=VMEM,
        out_shape=jax.ShapeDtypeStruct(parts.shape[1:], parts.dtype),
        compiler_params=LIMIT,
        name="fold",
    )(parts)


def adjoint_kernel(place_ref, gaps_ref, weighted_ref, green_ref, out_ref, flat, late, *, rows, nb):
    height, cells = out_ref.shape
    blocks, sensors, _ = green_ref.shape
    up = height // TALL
    lag = lags(place_ref, gaps_ref, blocks)
    flat[pl.ds(height, TALL), :] = jnp.zeros((TALL, sensors), flat.dtype)
    for q in range(up * (sensors // WIDE)):
        j, a = q // up, q % up
        block = weighted_ref[q]
        late[0, pl.ds(a * TALL, TALL), pl.ds(j * WIDE, WIDE)] = block
        flat[pl.ds(a * TALL, TALL), pl.ds(j * WIDE, WIDE)] = block.astype(jnp.float32)
    late[0, pl.ds(height, height), :] = jnp.zeros((height, sensors), late.dtype)
    late[1, pl.ds(0, height), :] = flat[pl.ds(rows, height), :].astype(late.dtype)
    late[1, pl.ds(height, height), :] = jnp.zeros((height, sensors), late.dtype)
    for part in range(blocks // nb):
        windows = []
        for k in range(part * nb, part * nb + nb):
            half = lax.shift_right_logical(lag[k], 1)
            start = pl.multiple_of(half * (2 * rows), 2 * rows)
            windows.append(late[lag[k] - 2 * half, pl.ds(start, height), :])
        held = green_ref[pl.ds(part * nb, nb)].reshape(nb * sensors, cells)
        value = jnp.dot(jnp.concatenate(windows, axis=1), held, preferred_element_type=jnp.float32)
        if part == 0:
            out_ref[...] = value.astype(out_ref.dtype)
        else:
            out_ref[...] = (out_ref[...] + value).astype(out_ref.dtype)


def adjoint(place, gaps, weighted, green, rows, steps, nb):
    blocks, sensors, cells = green.shape
    height = rows * steps
    return pl.pallas_call(
        functools.partial(adjoint_kernel, rows=rows, nb=nb),
        in_specs=[SMEM, SMEM, VMEM, VMEM],
        out_specs=VMEM,
        scratch_shapes=[
            pltpu.VMEM((height + TALL, sensors), jnp.float32),
            pltpu.VMEM((2, 2 * height, sensors), jnp.bfloat16),
        ],
        out_shape=jax.ShapeDtypeStruct((height, cells), jnp.float32),
        compiler_params=LIMIT,
        name="adjoint",
    )(place, gaps, weighted, green)


def body(green, source, observed, lag_gaps, huber_level):
    rows, steps, cells = source.shape
    sensors = green.shape[1]
    depth, owners, groups = lax.axis_size("z"), lax.axis_size(PLANE), lax.axis_size("y")
    place, owner = lax.axis_index("y")[None], lax.axis_index(PLANE)[None]

    level = huber_level.reshape(sensors // WIDE, WIDE)
    parts, side = forward(place, owner, lag_gaps, source, green, observed, level, owners, WIRE)
    parts = lax.all_to_all(parts, PLANE, 0, 0, tiled=True)
    cores = lax.axis_size("c")
    turned = [[(p + depth // 2) % depth * cores + c for p in range(depth)] for c in range(cores)]
    planes = plane_sum(parts, depth, WIRE)
    planes = lax.all_to_all(planes, ("z", "c"), 0, 0, axis_index_groups=turned, tiled=True)

    weighted = weigh(planes, side, owners)
    weighted = lax.all_to_all(weighted, PLANE, 0, 0, tiled=True)

    terms = adjoint(place, lag_gaps, weighted, green, rows, steps, 4)
    terms = terms.reshape(groups, steps // groups, rows, cells)
    terms = fold(lax.all_to_all(terms, "y", 0, 0, tiled=True))
    return terms.transpose(1, 0, 2)


def solution(mesh):
    fine = Mesh(mesh.devices.reshape(16, 4, 2, 4), ("z", "x", "c", "y"))
    cell = ("z", "x", "c")
    in_specs = (P("y", None, cell), P(None, None, cell), P(), P(), P())
    out_specs = P(None, "y", cell)
    return jax.shard_map(body, mesh=fine, in_specs=in_specs, out_specs=out_specs, check_vma=False)
```

```python
import functools
import jax
import jax.numpy as jnp
from jax import lax
from jax.experimental import pallas as pl
from jax.experimental.pallas import tpu as pltpu
from jax.sharding import Mesh, PartitionSpec as P

PLANE = ("x", "c", "y")
TALL, WIDE = 64, 128
WIRE = jnp.bfloat16
VMEM = pl.BlockSpec(memory_space=pltpu.VMEM)
SMEM = pl.BlockSpec(memory_space=pltpu.SMEM)
HBM = pl.BlockSpec(memory_space=pl.ANY)
LIMIT = pltpu.CompilerParams(vmem_limit_bytes=20 << 20)


def lags(place_ref, gaps_ref, own_count):
    before = place_ref[0] * own_count
    lag = jnp.int32(0)
    for i in range(gaps_ref.shape[0] - own_count + 1):
        lag = lag + jnp.where(i < before, gaps_ref[i], 0)
    found = [lag]
    for i in range(own_count - 1):
        lag = lag + gaps_ref[before + i]
        found.append(lag)
    return found


def forward_kernel(
    place_ref, owner_ref, gaps_ref, source_ref, green_ref, observed_ref, level_ref,
    out_ref, side_ref, gaps, source, green, early, seen, level, sems
):
    rows, steps, cells = source.shape
    blocks, sensors, _ = green.shape
    height = rows * steps
    up = height // TALL
    lanes = early.shape[2]
    gaps_in = pltpu.make_async_copy(gaps_ref, gaps, sems.at[0])
    source_in = pltpu.make_async_copy(source_ref, source, sems.at[1])
    gaps_in.start()
    source_in.start()
    green_in = pltpu.make_async_copy(green_ref, green, sems.at[2])
    green_in.start()
    own = jnp.minimum(owner_ref[0], up * (sensors // WIDE) - 1)
    column = lax.div(own, up)
    when = pl.ds(pl.multiple_of(lax.rem(own, up) * (TALL // rows), TALL // rows), TALL // rows)
    where = pl.ds(pl.multiple_of(column * WIDE, WIDE), WIDE)
    seen_in = pltpu.make_async_copy(observed_ref.at[:, when, where], seen, sems.at[3])
    seen_in.start()
    level_in = pltpu.make_async_copy(level_ref, level, sems.at[4])
    level_in.start()
    early[:, pl.ds(0, height), :] = jnp.zeros((early.shape[0], height, lanes), early.dtype)
    gaps_in.wait()
    lag = lags(place_ref, gaps, blocks)
    source_in.wait()
    for i in range(cells // lanes):
        for r in range(rows):
            piece = source[r, :, i * lanes:(i + 1) * lanes].astype(jnp.float32)
            early[i, pl.ds(height + r, steps, stride=rows), :] = piece

    shifted = []
    for k in range(blocks):
        start = pl.multiple_of((steps - lag[k]) * rows, rows)
        for i in range(cells // lanes):
            shifted.append(early[i, pl.ds(start, height), :].astype(jnp.bfloat16))
    green_in.wait()
    value = lax.dot_general(
        jnp.concatenate(shifted, axis=1), jnp.concatenate([green[k] for k in range(blocks)], axis=1),
        (((1,), (1,)), ((), ())), preferred_element_type=jnp.float32,
    )
    for q in range(out_ref.shape[0]):
        j, a = q // up, q % up
        if j < value.shape[1] // WIDE:
            block = value[a * TALL:(a + 1) * TALL, j * WIDE:(j + 1) * WIDE]
        else:
            block = jnp.zeros((TALL, WIDE), value.dtype)
        out_ref[q] = block.astype(out_ref.dtype)
    seen_in.wait()
    level_in.wait()
    tall = TALL // rows
    for r in range(rows):
        side_ref[pl.ds(r, tall, stride=rows), :] = seen[r]
    threshold = 0.3 * (level[pl.ds(column, 1), :].astype(jnp.float32) + 1.0)
    side_ref[pl.ds(TALL, 8), :] = jnp.broadcast_to(threshold, (8, WIDE))


def forward(place, owner, gaps, source, green, observed, level, owners, wire):
    rows, steps, cells = source.shape
    blocks, sensors, _ = green.shape
    height = rows * steps
    return pl.pallas_call(
        forward_kernel,
        in_specs=[SMEM, SMEM, HBM, HBM, HBM, HBM, HBM],
        out_specs=[VMEM, VMEM],
        scratch_shapes=[
            pltpu.SMEM(gaps.shape, gaps.dtype),
            pltpu.VMEM(source.shape, source.dtype),
            pltpu.VMEM(green.shape, green.dtype),
            pltpu.VMEM((pl.cdiv(cells, 128), 2 * height, min(cells, 128)), jnp.float32),
            pltpu.VMEM((rows, TALL // rows, WIDE), observed.dtype),
            pltpu.VMEM(level.shape, level.dtype),
            pltpu.SemaphoreType.DMA((5,)),
        ],
        out_shape=[
            pltpu.VMEM((owners, TALL, WIDE), wire),
            pltpu.VMEM((TALL + 8, WIDE), observed.dtype),
        ],
        name="forward",
    )(place, owner, gaps, source, green, observed, level)


def plane_kernel(parts_ref, out_ref):
    value = parts_ref[0].astype(jnp.float32)
    for q in range(1, parts_ref.shape[0]):
        value = value + parts_ref[q].astype(jnp.float32)
    value = value.astype(out_ref.dtype)
    for p in range(out_ref.shape[0]):
        out_ref[p] = value


def plane_sum(parts, copies, wire):
    return pl.pallas_call(
        plane_kernel,
        in_specs=[VMEM],
        out_specs=VMEM,
        out_shape=jax.ShapeDtypeStruct((copies,) + parts.shape[1:], wire),
        compiler_params=LIMIT,
        name="plane_sum",
    )(parts)


def weigh_kernel(parts_ref, side_ref, out_ref):
    value = parts_ref[0].astype(jnp.float32)
    for p in range(1, parts_ref.shape[0]):
        value = value + parts_ref[p].astype(jnp.float32)
    tall = parts_ref.shape[1]
    misfit = value - side_ref[pl.ds(0, tall), :]
    threshold = side_ref[pl.ds(tall, 1), :]
    weighted = (misfit * threshold / jnp.maximum(jnp.abs(misfit), threshold)).astype(out_ref.dtype)
    for q in range(out_ref.shape[0]):
        out_ref[q] = weighted


def weigh(parts, side, copies):
    return pl.pallas_call(
        weigh_kernel,
        in_specs=[VMEM, VMEM],
        out_specs=VMEM,
        out_shape=jax.ShapeDtypeStruct((copies,) + parts.shape[1:], jnp.bfloat16),
        compiler_params=LIMIT,
        name="weigh",
    )(parts, side)


def fold_kernel(parts_ref, out_ref):
    value = parts_ref[0]
    for y in range(1, parts_ref.shape[0]):
        value = value + parts_ref[y]
    out_ref[...] = value


def fold(parts):
    return pl.pallas_call(
        fold_kernel,
        in_specs=[VMEM],
        out_specs=VMEM,
        out_shape=jax.ShapeDtypeStruct(parts.shape[1:], parts.dtype),
        compiler_params=LIMIT,
        name="fold",
    )(parts)


def adjoint_kernel(place_ref, gaps_ref, weighted_ref, green_ref, out_ref, flat, late, *, rows, nb):
    height, cells = out_ref.shape
    blocks, sensors, _ = green_ref.shape
    up = height // TALL
    lag = lags(place_ref, gaps_ref, blocks)
    flat[pl.ds(height, TALL), :] = jnp.zeros((TALL, sensors), flat.dtype)
    for q in range(up * (sensors // WIDE)):
        j, a = q // up, q % up
        block = weighted_ref[q]
        late[0, pl.ds(a * TALL, TALL), pl.ds(j * WIDE, WIDE)] = block
        flat[pl.ds(a * TALL, TALL), pl.ds(j * WIDE, WIDE)] = block.astype(jnp.float32)
    late[0, pl.ds(height, height), :] = jnp.zeros((height, sensors), late.dtype)
    late[1, pl.ds(0, height), :] = flat[pl.ds(rows, height), :].astype(late.dtype)
    late[1, pl.ds(height, height), :] = jnp.zeros((height, sensors), late.dtype)
    for part in range(blocks // nb):
        windows = []
        for k in range(part * nb, part * nb + nb):
            half = lax.shift_right_logical(lag[k], 1)
            start = pl.multiple_of(half * (2 * rows), 2 * rows)
            windows.append(late[lag[k] - 2 * half, pl.ds(start, height), :])
        held = green_ref[pl.ds(part * nb, nb)].reshape(nb * sensors, cells)
        value = jnp.dot(jnp.concatenate(windows, axis=1), held, preferred_element_type=jnp.float32)
        if part == 0:
            out_ref[...] = value.astype(out_ref.dtype)
        else:
            out_ref[...] = (out_ref[...] + value).astype(out_ref.dtype)


def adjoint(place, gaps, weighted, green, rows, steps, nb):
    blocks, sensors, cells = green.shape
    height = rows * steps
    return pl.pallas_call(
        functools.partial(adjoint_kernel, rows=rows, nb=nb),
        in_specs=[SMEM, SMEM, VMEM, VMEM],
        out_specs=VMEM,
        scratch_shapes=[
            pltpu.VMEM((height + TALL, sensors), jnp.float32),
            pltpu.VMEM((2, 2 * height, sensors), jnp.bfloat16),
        ],
        out_shape=jax.ShapeDtypeStruct((height, cells), jnp.float32),
        compiler_params=LIMIT,
        name="adjoint",
    )(place, gaps, weighted, green)


def body(green, source, observed, lag_gaps, huber_level):
    rows, steps, cells = source.shape
    sensors = green.shape[1]
    depth, owners, groups = lax.axis_size("z"), lax.axis_size(PLANE), lax.axis_size("y")
    place, owner = lax.axis_index("y")[None], lax.axis_index(PLANE)[None]

    level = huber_level.reshape(sensors // WIDE, WIDE)
    parts, side = forward(place, owner, lag_gaps, source, green, observed, level, owners, WIRE)
    parts = lax.all_to_all(parts, PLANE, 0, 0, tiled=True)
    cores = lax.axis_size("c")
    turned = [[(p + depth // 2 + 2 * c) % depth * cores + c for p in range(depth)] for c in range(cores)]
    planes = plane_sum(parts, depth, WIRE)
    planes = lax.all_to_all(planes, ("z", "c"), 0, 0, axis_index_groups=turned, tiled=True)

    weighted = weigh(planes, side, owners)
    weighted = lax.all_to_all(weighted, PLANE, 0, 0, tiled=True)

    terms = adjoint(place, lag_gaps, weighted, green, rows, steps, 4)
    terms = terms.reshape(groups, steps // groups, rows, cells)
    terms = fold(lax.all_to_all(terms, "y", 0, 0, tiled=True))
    return terms.transpose(1, 0, 2)


def solution(mesh):
    fine = Mesh(mesh.devices.reshape(16, 4, 2, 4), ("z", "x", "c", "y"))
    cell = ("z", "x", "c")
    in_specs = (P("y", None, cell), P(None, None, cell), P(), P(), P())
    out_specs = P(None, "y", cell)
    return jax.shard_map(body, mesh=fine, in_specs=in_specs, out_specs=out_specs, check_vma=False)
```
